32 devices in a mesh: row: 8 (over z, y), col: 4 (over x, core).
Axes of the slice: x: 2, y: 2, z: 4, core: 2. Of those that a mesh axis runs over, the one named last changes fastest.
Arguments:
- query_acts: bfloat16 [256, 8192], P('col', 'row'), may hold values from -6 to 6
- query_grads: bfloat16 [256, 28672], P('row', 'col'), may hold values from -6 to 6
- ritz_mats: float32 [3, 8192, 28672], P(None, 'row', 'col'), may hold values from -0.095683193 to 0.095683193, as said below
- eigenvalues: float32 [3], replicated, may hold values from 0.5 to 4
- train_acts: bfloat16 [64, 8192], P('row'), may hold values from -6 to 6
- train_grads: bfloat16 [64, 28672], P('row', 'col'), may hold values from -6 to 6
Outputs:
- response: bfloat16 [64, 28672], P('row', 'col')
- scores: float32 [64], P('row')
The draws below stay inside these ranges and needn't reach their ends.
Inputs may be any that keep to these rules, and one draw needn't show every extreme that they name: `ritz_mats`: real entries of order one over the square root of 8192; every matrix has full rank.
All inputs are finite; a program needn't handle non-finite values.
Results may differ from the reference program's by a relative error of at most 0.0012.
Values may be sent and summed in bfloat16 or wider, within the bound.
No kernel may reach another device: no remote copies, remote signals or barrier semaphores. Data moves between devices by JAX's collectives and lax.ppermute only.
A program may use at most 192 MiB of HBM per device.

```python
import math
import jax
import jax.numpy as jnp
from jax import lax

D_IN = 8192
D_OUT = 28672
RITZ = 3
QUERY = 256
TRAIN = 64


def draw_ritz_mats(key, part):
    position = jnp.arange(D_IN, dtype=jnp.float32) / max(D_IN - 1, 1)
    entries = jnp.clip(jax.random.normal(key, (RITZ, D_IN, D_OUT), jnp.float32), -5.0, 5.0)
    factor = jnp.exp(math.log(3.0) * (position - 0.5))
    return entries * factor[None, :, None] / math.sqrt(D_IN)


def level_of(rng, shape, pieces, smallest, largest):
    loudness, own = 1.0, jax.random.fold_in(rng, 6)
    for dim, blocks in pieces:
        steps = jnp.exp(jax.random.uniform(jax.random.fold_in(own, dim), (blocks,), jnp.float32, smallest / len(pieces), largest / len(pieces)))
        loudness = loudness * jnp.repeat(steps, shape[dim] // blocks).reshape([-1 if axis == dim else 1 for axis in range(len(shape))])
    return loudness


def noise(stream_key, dims, width, limit, shards=(), held_as=jnp.bfloat16):
    gain = level_of(stream_key, dims, shards, -0.22, 0.18) if shards else 1.0
    values = jax.random.normal(stream_key, dims, jnp.float32) * width * gain
    return jnp.minimum(jnp.maximum(values, -limit), limit).astype(held_as)


def setup_inputs(seed: int = 0) -> dict:
    key_list = jax.random.split(jax.random.key(seed), 7)
    return {
        "query_acts": noise(key_list[0], (QUERY, D_IN), 1.0, 6.0, ((0, 4), (1, 8))),
        "query_grads": noise(key_list[1], (QUERY, D_OUT), 1.0, 6.0, ((0, 8), (1, 4))),
        "ritz_mats": draw_ritz_mats(jax.random.fold_in(key_list[6], 71), 0),
        "eigenvalues": jnp.clip(jnp.exp(jax.random.uniform(key_list[3], (RITZ,), jnp.float32, math.log(0.5), math.log(4.0))), 0.5, 4.0),
        "train_acts": noise(key_list[4], (TRAIN, D_IN), 1.0, 6.0, ((0, 8),)),
        "train_grads": noise(key_list[5], (TRAIN, D_OUT), 1.0, 6.0, ((0, 8), (1, 4))),
    }


def reference(query_acts, query_grads, ritz_mats, eigenvalues, train_acts, train_grads):
    highest = lax.Precision.HIGHEST
    query_gradient = jnp.dot(query_acts.T, query_grads, preferred_element_type=jnp.float32)

    def project(matrix):
        return jnp.sum(matrix * query_gradient)
    coeffs = lax.map(project, ritz_mats)
    weights = coeffs / (eigenvalues * math.sqrt(QUERY * D_OUT))
    combined = jnp.tensordot(weights, ritz_mats, axes=1, precision=highest)
    response_full = jnp.dot(train_acts.astype(jnp.float32), combined, precision=highest)
    response = response_full.astype(jnp.bfloat16)
    scores = lax.optimization_barrier(jnp.sum(response_full * train_grads.astype(jnp.float32), axis=1)) / math.sqrt(D_OUT)
    return (response, scores)
```

```python
import functools
import math

import jax
import jax.numpy as jnp
from jax import lax
from jax.experimental import pallas as pl
from jax.experimental.pallas import tpu as pltpu
from jax.sharding import PartitionSpec as P


LANES = 128
TILE = 256
CHUNKS = (7, 7, 7, 7)


def pass_kernel(n_pieces, depth, x_ref, at_ref, *refs):
    g_refs = refs[:n_pieces]
    r_ref, t_ref, c_ref = refs[n_pieces:]
    g = jnp.concatenate([ref[...] for ref in g_refs], axis=0)
    n_ritz, rows, width = r_ref.shape
    tokens = x_ref.shape[0]

    @pl.when(pl.program_id(0) == 0)
    def _():
        c_ref[...] = jnp.zeros_like(c_ref)

    totals = [jnp.zeros((tokens, width), jnp.float32) for _ in range(n_ritz)]
    sums = [jnp.zeros((8, width), jnp.float32) for _ in range(n_ritz)]
    for start in range(0, rows, depth):
        block = slice(start, start + depth)
        q = jnp.dot(at_ref[block, :], g, preferred_element_type=jnp.float32)
        x = x_ref[:, block]
        for k in range(n_ritz):
            r = r_ref[k, block, :]
            sums[k] += jnp.sum((r * q).reshape(depth // 8, 8, width), axis=0)
            high = r.astype(jnp.bfloat16)
            low = (r - high.astype(jnp.float32)).astype(jnp.bfloat16)
            totals[k] += jnp.dot(x, high, preferred_element_type=jnp.float32)
            totals[k] += jnp.dot(x, low, preferred_element_type=jnp.float32)
    for k in range(n_ritz):
        t_ref[k] = totals[k]
        part = sums[k][:, :LANES]
        for lane in range(LANES, width, LANES):
            part += sums[k][:, lane : lane + LANES]
        c_ref[k] += part


def one_pass(x, at, pieces, offsets, ritz, offset, width):
    n_ritz, rows, _ = ritz.shape
    tokens = x.shape[0]
    depth = min(256, rows)
    first = offset // TILE

    def columns(start):
        return lambda j: (0, start // TILE + j)

    specs = [
        pl.BlockSpec((piece.shape[0], TILE), columns(start)) for piece, start in zip(pieces, offsets)
    ]
    queries = at.shape[1]
    return pl.pallas_call(
        functools.partial(pass_kernel, len(pieces), depth),
        grid=(width // TILE,),
        in_specs=[
            pl.BlockSpec((tokens, rows), lambda j: (0, 0)),
            pl.BlockSpec((rows, queries), lambda j: (0, 0)),
            *specs,
            pl.BlockSpec((n_ritz, rows, TILE), lambda j: (0, 0, first + j)),
        ],
        out_specs=[
            pl.BlockSpec((n_ritz, tokens, TILE), lambda j: (0, 0, j)),
            pl.BlockSpec((n_ritz, 8, LANES), lambda j: (0, 0, 0)),
        ],
        out_shape=[
            jax.ShapeDtypeStruct((n_ritz, tokens, width), jnp.float32),
            jax.ShapeDtypeStruct((n_ritz, 8, LANES), jnp.float32),
        ],
        compiler_params=pltpu.CompilerParams(
            dimension_semantics=("arbitrary",), vmem_limit_bytes=40 * 2**20
        ),
        cost_estimate=pl.CostEstimate(
            flops=2 * rows * width * (queries + 2 * n_ritz * tokens),
            bytes_accessed=n_ritz * rows * width * 4,
            transcendentals=0,
        ),
        name="one_pass",
    )(x, at, *pieces, ritz)


def mix_kernel(share, w_ref, place_ref, t_ref, keep_ref, send_ref):
    z, y = place_ref[0], place_ref[1]
    n_ritz = t_ref.shape[0]
    for slot in range(keep_ref.shape[0]):
        for ref, side in ((keep_ref, y), (send_ref, 1 - y)):
            start = pl.multiple_of((2 * (z ^ slot) + side) * share, share)
            total = w_ref[0] * t_ref[0, pl.ds(start, share), :]
            for k in range(1, n_ritz):
                total += w_ref[k] * t_ref[k, pl.ds(start, share), :]
            ref[slot] = total


def mix(weights, place, terms, lines):
    n_ritz, tokens, width = terms.shape
    share = tokens // (2 * lines)
    out = jax.ShapeDtypeStruct((lines, share, width), jnp.float32)
    return pl.pallas_call(
        functools.partial(mix_kernel, share),
        in_specs=[
            pl.BlockSpec(memory_space=pltpu.SMEM),
            pl.BlockSpec(memory_space=pltpu.SMEM),
            pl.BlockSpec(memory_space=pltpu.VMEM),
        ],
        out_specs=[pl.BlockSpec(memory_space=pltpu.VMEM)] * 2,
        out_shape=[out, out],
        cost_estimate=pl.CostEstimate(
            flops=2 * terms.size, bytes_accessed=5 * terms.size, transcendentals=0
        ),
        name="mix",
    )(weights, place, terms)


def swap(value, mask):
    size = lax.axis_size("row")
    return lax.ppermute(value, "row", [(i, i ^ mask) for i in range(size)])


def sum_everywhere(value):
    size = lax.axis_size("row") * lax.axis_size("col")
    block = jnp.zeros((8, LANES), jnp.float32).at[0, : value.shape[0]].set(value)
    mine = jnp.broadcast_to(block[None], (size, 8, LANES))
    theirs = lax.all_to_all(mine, ("row", "col"), 0, 0)
    return jnp.sum(theirs, axis=0)[0, : value.shape[0]]


def per_device(query_acts, query_grads, ritz_mats, eigenvalues, train_acts, train_grads, *, d_out):
    n_row = lax.axis_size("row")
    width = ritz_mats.shape[2]
    acts_all = lax.all_gather(query_acts, "col", axis=0, tiled=True)
    queries = acts_all.shape[0]
    scale = eigenvalues * math.sqrt(queries * d_out)
    root_width = math.sqrt(d_out)
    x = lax.all_to_all(train_acts, "row", split_axis=1, concat_axis=0, tiled=True)

    if n_row != 8 or width != TILE * sum(CHUNKS):
        grads_all = lax.all_gather(query_grads, "row", axis=0, tiled=True)
        terms, parts = one_pass(x, acts_all.T, [grads_all], [0], ritz_mats, 0, width)
        coeffs = lax.psum(jnp.sum(parts, axis=(1, 2)), ("row", "col"))
        weights = coeffs / scale
        total = weights[0] * terms[0]
        for k in range(1, terms.shape[0]):
            total = total + weights[k] * terms[k]
        response_full = lax.psum_scatter(total, "row", scatter_dimension=0, tiled=True)
        score_terms = jnp.sum(response_full * train_grads.astype(jnp.float32), axis=1)
        scores = lax.psum(score_terms / root_width, "col")
        return response_full.astype(jnp.bfloat16), scores

    lines = n_row // 2
    me = lax.axis_index("row")
    z, y = me // 2, me % 2
    share = query_grads.shape[0]
    order = [(z ^ m) * 2 + side for side in (y, 1 - y) for m in range(lines)]
    at = jnp.concatenate(
        [lax.dynamic_slice_in_dim(acts_all, r * share, share, 0) for r in order], axis=0
    ).T

    terms, parts = [], []
    offset = 0
    for tiles in CHUNKS:
        size = tiles * TILE
        mine = query_grads[:, offset : offset + size]
        line = [mine] + [swap(mine, 2 * m) for m in range(1, lines)]
        across = [swap(piece, 1) for piece in line]
        t, c = one_pass(
            x,
            at,
            [query_grads, *line[1:], *across],
            [offset] + [0] * (2 * lines - 1),
            ritz_mats,
            offset,
            size,
        )
        terms.append(t)
        parts.append(c)
        offset += size
    coeffs = sum_everywhere(jnp.sum(sum(parts), axis=(1, 2)))
    weights = coeffs / scale
    place = jnp.stack([z, y]).astype(jnp.int32)

    responses, score_terms = [], 0.0
    offset = 0
    for t in terms:
        size = t.shape[2]
        keep, send = mix(weights, place, t, lines)
        held = keep + swap(send, 1)
        total = held[0]
        for m in range(1, lines):
            total = total + swap(held[m], 2 * m)
        responses.append(total.astype(jnp.bfloat16))
        grads = train_grads[:, offset : offset + size].astype(jnp.float32)
        score_terms = score_terms + jnp.sum(total * grads, axis=1)
        offset += size
    scores = lax.psum(score_terms / root_width, "col")
    return jnp.concatenate(responses, axis=1), scores


def solution(mesh):
    in_specs = (
        P("col", "row"),
        P("row", "col"),
        P(None, "row", "col"),
        P(),
        P("row", None),
        P("row", "col"),
    )
    out_specs = (P("row", "col"), P("row"))

    def program(query_acts, query_grads, ritz_mats, eigenvalues, train_acts, train_grads):
        body = functools.partial(per_device, d_out=ritz_mats.shape[2])
        return jax.shard_map(
            body, mesh=mesh, in_specs=in_specs, out_specs=out_specs, check_vma=False
        )(query_acts, query_grads, ritz_mats, eigenvalues, train_acts, train_grads)

    return program
```

```python
import functools
import math

import jax
import jax.numpy as jnp
from jax import lax
from jax.experimental import pallas as pl
from jax.experimental.pallas import tpu as pltpu
from jax.sharding import PartitionSpec as P


LANES = 128
TILE = 1024
ROWS = 512
SUB = 256
CHUNKS = (1, 2, 2, 2)
EARLY = 2


def pass_kernel(lines, n_pieces, x_ref, at_ref, *refs):
    g_refs = refs[:n_pieces]
    r_ref, keep_ref, send_ref, c_ref, g_buf, t_buf = refs[n_pieces:]
    n_ritz, rows, width = r_ref.shape
    tokens = x_ref.shape[0]
    block = pl.program_id(1)

    me = lax.axis_index("row")
    z, y = me // 2, me % 2
    slots = [(z ^ m) * 2 + side for side in (y, 1 - y) for m in range(lines)]
    col = lax.axis_index("col")
    homes = [(z ^ m ^ col) * 2 + side for side in (y, 1 - y) for m in range(lines)]

    @pl.when((pl.program_id(0) == 0) & (block == 0))
    def _():
        c_ref[...] = jnp.zeros_like(c_ref)

    @pl.when(block == 0)
    def _():
        t_buf[...] = jnp.zeros_like(t_buf)
        if not lines:
            g_buf[...] = g_refs[0][...]
        else:
            share = g_buf.shape[0] // len(homes)
            todo = iter(homes)
            for ref in g_refs:
                for at in range(0, ref.shape[0], share):
                    start = pl.multiple_of(next(todo) * share, share)
                    g_buf[pl.ds(start, share), :] = ref[at : at + share, :]

    first = pl.multiple_of(block * rows, rows)
    a = at_ref[pl.ds(first, rows), :]
    x = x_ref[:, pl.ds(first, rows)]
    for lane in range(0, width, SUB):
        cols = slice(lane, lane + SUB)
        q = jnp.dot(a, g_buf[:, cols], preferred_element_type=jnp.float32)
        for k in range(n_ritz):
            r = r_ref[k, :, cols]
            part = jnp.sum((r * q).reshape(rows // 8, 8, SUB), axis=0)
            for at in range(0, SUB, LANES):
                c_ref[k] += part[:, at : at + LANES]
            high = r.astype(jnp.bfloat16)
            low = (r - high.astype(jnp.float32)).astype(jnp.bfloat16)
            t_buf[k, :, cols] += jnp.dot(x, high, preferred_element_type=jnp.float32) + jnp.dot(
                x, low, preferred_element_type=jnp.float32
            )

    @pl.when(block == pl.num_programs(1) - 1)
    def _():
        if not lines:
            keep_ref[...] = t_buf[:, : tokens // 2, :]
            send_ref[...] = t_buf[:, tokens // 2 :, :]
        else:
            share = tokens // len(slots)
            for n, slot in enumerate(slots):
                ref = keep_ref if n < lines else send_ref
                at = n % lines * share
                start = pl.multiple_of(slot * share, share)
                ref[:, at : at + share, :] = t_buf[:, pl.ds(start, share), :]


def one_pass(lines, x, at, pieces, offsets, ritz, offset, width, tile):
    n_ritz, rows, _ = ritz.shape
    tokens = x.shape[0]
    depth = min(ROWS, rows)
    first = offset // tile
    queries = at.shape[1]

    def columns(start):
        return lambda j, i: (0, start // tile + j)

    specs = [
        pl.BlockSpec((piece.shape[0], tile), columns(start)) for piece, start in zip(pieces, offsets)
    ]
    half = pl.BlockSpec((n_ritz, tokens // 2, tile), lambda j, i: (0, 0, j))
    return pl.pallas_call(
        functools.partial(pass_kernel, lines, len(pieces)),
        grid=(width // tile, rows // depth),
        in_specs=[
            pl.BlockSpec((tokens, rows), lambda j, i: (0, 0)),
            pl.BlockSpec((rows, queries), lambda j, i: (0, 0)),
            *specs,
            pl.BlockSpec((n_ritz, depth, tile), lambda j, i: (0, i, first + j)),
        ],
        out_specs=[
            half,
            half,
            pl.BlockSpec((n_ritz, 8, LANES), lambda j, i: (0, 0, 0)),
        ],
        out_shape=[
            jax.ShapeDtypeStruct((n_ritz, tokens // 2, width), jnp.float32),
            jax.ShapeDtypeStruct((n_ritz, tokens // 2, width), jnp.float32),
            jax.ShapeDtypeStruct((n_ritz, 8, LANES), jnp.float32),
        ],
        scratch_shapes=[
            pltpu.VMEM((queries, tile), jnp.bfloat16),
            pltpu.VMEM((n_ritz, tokens, tile), jnp.float32),
        ],
        compiler_params=pltpu.CompilerParams(
            dimension_semantics=("arbitrary", "arbitrary"), vmem_limit_bytes=28 * 2**20
        ),
        cost_estimate=pl.CostEstimate(
            flops=2 * rows * width * (queries + 2 * n_ritz * tokens),
            bytes_accessed=n_ritz * rows * width * 4,
            transcendentals=0,
        ),
        name="one_pass",
    )(x, at, *pieces, ritz)


def swap(value, mask, axis="row"):
    size = lax.axis_size(axis)
    return lax.ppermute(value, axis, [(i, i ^ mask) for i in range(size)])


def sum_everywhere(parts):
    size = lax.axis_size("row") * lax.axis_size("col")
    block = jnp.pad(parts, ((0, 8 - parts.shape[0]), (0, 0)))
    mine = jnp.broadcast_to(block[None], (size, *block.shape))
    theirs = lax.all_to_all(mine, ("row", "col"), 0, 0)
    return jnp.sum(theirs, axis=(0, 2))[: parts.shape[0]]


def blend(weights, terms):
    total = weights[0] * terms[0]
    for k in range(1, terms.shape[0]):
        total = total + weights[k] * terms[k]
    return total


def blend_kernel(n_terms, n_add, w_ref, *refs):
    terms, adds, outs = refs[:n_terms], refs[n_terms : n_terms + n_add], refs[n_terms + n_add :]
    total = None
    for k in range(terms[0].shape[0]):
        value = terms[0][k]
        for ref in terms[1:]:
            value = value + ref[k]
        total = w_ref[k] * value if total is None else total + w_ref[k] * value
    for ref in adds:
        total = total + ref[...]
    share = outs[0].shape[0]
    for n, ref in enumerate(outs):
        ref[...] = total[n * share : (n + 1) * share]


def blended(weights, terms, adds, pieces):
    n_ritz, tokens, width = terms[0].shape
    share = tokens // pieces
    tile = min(width, TILE)
    return pl.pallas_call(
        functools.partial(blend_kernel, len(terms), len(adds)),
        grid=(width // tile,),
        in_specs=[pl.BlockSpec(memory_space=pltpu.SMEM)]
        + [pl.BlockSpec((n_ritz, tokens, tile), lambda j: (0, 0, j))] * len(terms)
        + [pl.BlockSpec((tokens, tile), lambda j: (0, j))] * len(adds),
        out_specs=[pl.BlockSpec((share, tile), lambda j: (0, j))] * pieces,
        out_shape=[jax.ShapeDtypeStruct((share, width), jnp.float32)] * pieces,
        compiler_params=pltpu.CompilerParams(
            dimension_semantics=("arbitrary",), vmem_limit_bytes=8 * 2**20
        ),
        cost_estimate=pl.CostEstimate(
            flops=2 * len(terms) * terms[0].size,
            bytes_accessed=4 * len(terms) * terms[0].size,
            transcendentals=0,
        ),
        name="blended",
    )(weights, *terms, *adds)


def per_device(query_acts, query_grads, ritz_mats, eigenvalues, train_acts, train_grads, *, d_out):
    n_row, n_col = lax.axis_size("row"), lax.axis_size("col")
    width = ritz_mats.shape[2]
    scale = eigenvalues * math.sqrt(n_col * query_acts.shape[0] * d_out)
    root_width = math.sqrt(d_out)

    if not chunked(n_row, n_col):
        x = lax.all_to_all(train_acts, "row", split_axis=1, concat_axis=0, tiled=True)
        acts_all = lax.all_gather(query_acts, "col", axis=0, tiled=True)
        grads_all = lax.all_gather(query_grads, "row", axis=0, tiled=True)
        first, second, parts = one_pass(
            0, x, acts_all.T, [grads_all], [0], ritz_mats, 0, width, 512
        )
        coeffs = lax.psum(jnp.sum(parts, axis=(1, 2)), ("row", "col"))
        total = blend(coeffs / scale, jnp.concatenate([first, second], axis=1))
        response_full = lax.psum_scatter(total, "row", scatter_dimension=0, tiled=True)
        score_terms = jnp.sum(response_full * train_grads.astype(jnp.float32), axis=1)
        scores = lax.psum(score_terms / root_width, "col")
        return response_full.astype(jnp.bfloat16), scores

    lines = n_row // 2
    x = lax.all_to_all(train_acts, "row", split_axis=1, concat_axis=0, tiled=True)
    acts = [query_acts] + [swap(query_acts, m, "col") for m in range(1, n_col)]
    at = jnp.concatenate(acts, axis=0).T
    line, offsets = [], []
    offset = 0
    for n, tiles in enumerate(CHUNKS):
        piece = query_grads[:, offset : offset + tiles * TILE]
        line.append([swap(piece, 2 * m) for m in range(1, lines)])
        if n == 0:
            partner = swap(query_grads, 1)
        offsets.append(offset)
        offset += tiles * TILE

    keeps, sends, parts = [], [], []
    for n, tiles in enumerate(CHUNKS):
        across = swap(jnp.concatenate(line[n], axis=0), 1)
        keep, send, part = one_pass(
            lines,
            x,
            at,
            [query_grads, *line[n], partner, across],
            [offsets[n], 0, 0, 0, offsets[n], 0],
            ritz_mats,
            offsets[n],
            tiles * TILE,
            TILE,
        )
        if n < EARLY:
            send = swap(send, 1)
        keeps.append(keep)
        sends.append(send)
        parts.append(part)
    coeffs = sum_everywhere(jnp.sum(sum(parts), axis=1))
    weights = coeffs / scale

    theirs = {}
    for n in range(EARLY, len(CHUNKS)):
        theirs[n] = swap(blended(weights, [sends[n]], [], 1)[0], 1)
    responses, score_terms = [], 0.0
    for n, tiles in enumerate(CHUNKS):
        if n < EARLY:
            held = blended(weights, [keeps[n], sends[n]], [], lines)
        else:
            held = blended(weights, [keeps[n]], [theirs[n]], lines)
        total = held[0]
        for m in range(1, lines):
            total = total + swap(held[m], 2 * m)
        responses.append(total.astype(jnp.bfloat16))
        grads = train_grads[:, offsets[n] : offsets[n] + tiles * TILE].astype(jnp.float32)
        score_terms = score_terms + jnp.sum(total * grads, axis=1)
    scores = lax.psum(score_terms / root_width, "col")
    return jnp.concatenate(responses, axis=1), scores


def chunked(n_row, n_col):
    return n_row == 8 and n_col == 4


def solution(mesh):
    in_specs = (
        P("col", "row"),
        P("row", "col"),
        P(None, "row", "col"),
        P(),
        P("row", None),
        P("row", "col"),
    )
    out_specs = (P("row", "col"), P("row"))

    def program(query_acts, query_grads, ritz_mats, eigenvalues, train_acts, train_grads):
        body = functools.partial(per_device, d_out=ritz_mats.shape[2])
        return jax.shard_map(
            body, mesh=mesh, in_specs=in_specs, out_specs=out_specs, check_vma=False
        )(query_acts, query_grads, ritz_mats, eigenvalues, train_acts, train_grads)

    return program
```
